256 devices in a mesh: sec: 8 (over x, core), term: 32 (over y, z).
Axes of the slice: x: 4, y: 4, z: 8, core: 2. Of those that a mesh axis runs over, the one named last changes fastest.
Arguments:
- env_blocks: bfloat16 [32, 16, 256, 256], P('term', 'sec'), may hold values from -6 to 6
- core_blocks: bfloat16 [512, 256, 256], P('sec', 'term'), may hold values from -0.375 to 0.375
- mpo_coeffs: bfloat16 [32, 32, 512], P(None, None, 'sec'), may hold values from -1 to 1
- pair_left: int32 [512], P('sec'), may hold values from 0 to 1
- pair_right: int32 [512], P('sec'), may hold values from 0 to 15
- block_dims: int32 [16], replicated, may hold values from 1 to 256, 3072 in all
Outputs:
- new_env: float32 [32, 16, 256, 256], P('term', 'sec')
The draws below stay inside these ranges and needn't reach their ends.
Inputs may be any that keep to these rules, and one draw needn't show every extreme that they name: `pair_left`: A pair's left block is one of the 2 blocks of the sec index that holds the pair.
All inputs are finite; a program needn't handle non-finite values.
Results may differ from the reference program's by a relative error of at most 0.004.
Values may be sent and summed in bfloat16 or wider, within the bound.
A program may use at most 128 MiB of HBM per device.

```python
import math
import jax
import jax.numpy as jnp
import numpy as np
from jax import lax

BLK = 256
NB_DEV = 2
PAIR_DEV = 64
NB = 16
PAIRS = 512
W = 32


def touch_ends(entries, rng, low, high):
    place = [jax.random.randint(jax.random.fold_in(rng, axis), (), 0, length) for axis, length in enumerate(entries.shape)]
    main_axis = entries.shape.index(max(entries.shape))
    next_to = place[:main_axis] + [(place[main_axis] + 1) % entries.shape[main_axis]] + place[main_axis + 1:]
    return entries.at[tuple(place)].set(low).at[tuple(next_to)].set(high)


def shard_levels(own_key, shape, split, smallest, high):
    def one(position, parts):
        heights = jax.random.uniform(jax.random.fold_in(jax.random.fold_in(own_key, 6), position), (parts,), jnp.float32, smallest / len(split), high / len(split))
        return jnp.repeat(jnp.exp(heights), shape[position] // parts).reshape((-1,) + (1,) * (len(shape) - position - 1))

    gain = one(*split[0])
    for cut in split[1:]:
        gain = gain * one(*cut)
    return gain


def length_profile(count, total, most, lean):
    weights = [(1 << 20) // math.isqrt(grade ** lean) + 1 for grade in range(2, count + 1)]
    rest, holding = total - most - (count - 1), [1] * (count - 1)
    while rest > 0:
        movable = [i for i in range(count - 1) if holding[i] < most]
        pool, budget = sum([weights[i] for i in movable]), rest
        for i in movable:
            more = min(most - holding[i], max(1, budget * weights[i] // pool), rest)
            holding[i] = holding[i] + more
            rest = rest - more
    return np.array([most] + holding)


def ragged(stream_key, number_of, total, limit, skew):
    if number_of == 2:
        one = jax.random.randint(stream_key, (), max(1, total - limit), min(limit, total - 1) + 1)
        return jnp.stack([one, total - one])
    tallies = jnp.asarray(length_profile(number_of, total, limit, skew), jnp.int32)
    couples = (number_of - 1) // 2
    giver, sink = tallies[1:1 + 2 * couples:2], tallies[2:2 + 2 * couples:2]
    slack = jnp.minimum(giver - 1, limit - sink)
    shifted = jax.random.randint(jax.random.fold_in(stream_key, 1), (couples,), 0, 1 << 20) % (slack + 1)
    tallies = tallies.at[1:1 + 2 * couples:2].set(giver - shifted).at[2:2 + 2 * couples:2].set(sink + shifted)
    return tallies[jax.random.permutation(jax.random.fold_in(stream_key, 2), number_of)]


def normal_values(stream_key, dims, spread, limit, shards=(), held_as=jnp.bfloat16):
    values = spread * jax.random.normal(stream_key, dims, jnp.float32)
    if shards:
        values = values * shard_levels(stream_key, dims, shards, -0.22, 0.18)
    return jnp.clip(values, -limit, limit).astype(held_as)


def setup_inputs(seed: int = 0) -> dict:
    key_of = jax.random.split(jax.random.key(seed), 7)
    env_blocks = normal_values(key_of[0], (W, NB, BLK, BLK), 1.0, 6.0, ((0, 32), (1, 8)))
    core_blocks = normal_values(key_of[1], (PAIRS, BLK, BLK), BLK ** -0.5, 0.375, ((0, 8), (1, 32)))
    mpo_coeffs = normal_values(key_of[2], (W, W, PAIRS), W ** -0.5, 1.0, ((2, 8),))
    pair_left = touch_ends(jax.random.randint(key_of[3], (PAIRS,), 0, NB_DEV), jax.random.fold_in(key_of[3], 1), 0, NB_DEV - 1).astype(jnp.int32)
    pair_right = touch_ends(jax.random.randint(key_of[4], (PAIRS,), 0, NB), jax.random.fold_in(key_of[4], 1), 0, NB - 1).astype(jnp.int32)
    block_dims = ragged(key_of[5], NB, NB * BLK * 3 // 4, BLK, 0).astype(jnp.int32)
    return {"env_blocks": env_blocks, "core_blocks": core_blocks, "mpo_coeffs": mpo_coeffs, "pair_left": pair_left, "pair_right": pair_right, "block_dims": block_dims}


def reference(env_blocks, core_blocks, mpo_coeffs, pair_left, pair_right, block_dims):
    rows = jnp.arange(BLK).astype(jnp.int32)
    left_all = ((jnp.arange(PAIRS).astype(jnp.int32) // PAIR_DEV) * NB_DEV + pair_left).astype(jnp.int32)
    coeff_pairs = jnp.moveaxis(mpo_coeffs, 2, 0)

    def one_pair(carry, items):
        core, left_block, right_block, coeff = items
        dim_left = block_dims[left_block]
        dim_right = block_dims[right_block]
        keep = (rows < dim_left)[:, None] & (rows < dim_right)[None, :]
        masked = jnp.where(keep, core, jnp.zeros((), core.dtype))
        envs = lax.dynamic_index_in_dim(env_blocks, left_block, 1, keepdims=False)
        mixed = jnp.einsum('wv,wrc->vrc', coeff.astype(jnp.float32), envs.astype(jnp.float32)).astype(jnp.bfloat16)
        half = jnp.einsum('vrc,cd->vrd', mixed.astype(jnp.float32), masked.astype(jnp.float32)).astype(jnp.bfloat16)
        term = jnp.einsum('rc,vrd->vcd', masked.astype(jnp.float32), half.astype(jnp.float32))
        carry = carry.at[:, right_block].add(term)
        return carry, None

    start = jnp.zeros((W, NB, BLK, BLK), jnp.float32)
    result, _ = lax.scan(one_pair, start, (core_blocks, left_all, pair_right, coeff_pairs))
    return result
```

```python
import jax
import jax.numpy as jnp
from jax import lax
from jax.experimental import pallas as pl
from jax.experimental.pallas import tpu as pltpu
from jax.sharding import PartitionSpec as P

MESH = pl.DeviceIdType.MESH
PAIRS = 64
ROWS = 64
ENV = tuple(range(0, 256, ROWS))
CORE = ((0, 16), (16, 16), (32, 16), (48, 8), (56, 8))
STAGES = len(ENV) + len(CORE)
BLK = 256
F32, BF16 = jnp.float32, jnp.bfloat16


def rem(a, n):
    return lax.rem(a + n, n)


def kernel(
    env_in, core_in, w_in, meta_in, fin_f, fin_z,
    env_all, core_all, mixed, run, kron, wbuf, mbuf, mscal,
    obuf, r1, r2m, r2p, fin_s, zs,
    rs, ds, dss, ss, own, own_s, meta_r, meta_s, sc_sem,
    xr1, xrm, xrp, xs, fr, fd, fs,
):
    sec, term = lax.axis_index("sec"), lax.axis_index("term")
    x, c, y, z = sec // 2, lax.rem(sec, 2), term // 8, lax.rem(term, 8)
    par = lax.rem(z, 2)
    z1 = z + 1 - 2 * par
    other = 1 - c
    role = lax.rem(c + par, 2)
    zr = z + role * (1 - 2 * par)
    t_own, t_role = 8 * y + z, 8 * y + zr

    def dev(x_=None, y_=None, z_=None, c_=None):
        x_ = x if x_ is None else x_
        y_ = y if y_ is None else y_
        z_ = z if z_ is None else z_
        c_ = c if c_ is None else c_
        return {"sec": 2 * x_ + c_, "term": 8 * y_ + z_}

    partner = dev(c_=other)
    near = {
        ("z", 1): dev(z_=rem(z + 2, 8)), ("z", -1): dev(z_=rem(z - 2, 8)),
        ("y", 1): dev(y_=rem(y + 1, 4)), ("y", -1): dev(y_=rem(y - 1, 4)),
        ("x", 1): dev(x_=rem(x + 1, 4)), ("x", -1): dev(x_=rem(x - 1, 4)),
    }
    across = [dev(z_=z1, c_=0), dev(z_=z1, c_=1)]
    swap = dev(z_=z1, c_=other)

    barrier = pltpu.get_barrier_semaphore()
    greet = [partner, *near.values(), *across]
    for who in greet:
        pl.semaphore_signal(barrier, inc=1, device_id=who, device_id_type=MESH)
    pl.semaphore_wait(barrier, len(greet))

    def remote(src, dst, send, recv, who):
        return pltpu.make_async_remote_copy(
            src_ref=src, dst_ref=dst, send_sem=send, recv_sem=recv,
            device_id=who, device_id_type=MESH,
        )

    def shard(i, t, whole):
        if i < len(ENV):
            rows = pl.ds(ENV[i], ROWS)
            return whole[0].at[t, :, rows, :] if t is not None else whole[0].at[:, rows, :]
        some = pl.ds(*CORE[i - len(ENV)])
        if t is None:
            return whole[1].at[some]
        return whole[1].at[some, pl.ds(pl.multiple_of(8 * t, 8), 8), :]

    held, given = (env_all, core_all), (env_in, core_in)

    def place_own(stages):
        @pl.when(role == 0)
        def _():
            for i in stages:
                pltpu.make_async_copy(shard(i, None, given), shard(i, t_own, held), own.at[i]).start()

        @pl.when(role == 1)
        def _():
            for i in stages:
                remote(shard(i, None, given), shard(i, t_own, held), own_s.at[i], own.at[i], swap).start()

    DIMS = (("z", "y"), ("y", "z"))
    OFFS = (0, -1, 1, 2)

    def piece(i, color, half, off1, off2):
        dz, dy = (off1, off2) if color == 0 else (off2, off1)
        t = 8 * rem(y + dy, 4) + rem(zr + 2 * dz + 8, 8)
        first, count = (ENV[i], ROWS) if i < len(ENV) else CORE[i - len(ENV)]
        first, count = (first, 3 * count // 4) if color == 0 else (first + 3 * count // 4, count // 4)
        if i < len(ENV):
            rows = pl.ds(first, count)
            return env_all.at[t, :, rows, :] if half is None else env_all.at[t, half, rows, :]
        if half is not None:
            count //= 2
            first += half * count
        return core_all.at[pl.ds(first, count), pl.ds(pl.multiple_of(8 * t, 8), 8), :]

    def send(i, color, half, off1, off2, dim, sign, slot):
        ref = piece(i, color, half, off1, off2)
        remote(ref, ref, ss.at[i], rs.at[i, color, slot], near[dim, sign]).start()

    def take(i, color, half, off1, off2, slot):
        ref = piece(i, color, half, off1, off2)
        remote(ref, ref, ss.at[i], rs.at[i, color, slot], partner).wait_recv()

    def share(i, color, half, off1, off2):
        ref = piece(i, color, half, off1, off2)
        remote(ref, ref, dss.at[i], ds.at[i], partner).start()

    def start_own(i):
        pltpu.make_async_copy(shard(i, None, given), shard(i, t_role, held), own.at[i]).wait()
        for color, (d1, d2) in enumerate(DIMS):
            send(i, color, None, 0, 0, d1, 1, 0)
            send(i, color, None, 0, 0, d1, -1, 1)
            send(i, color, None, 0, 0, d2, 1, 4)
            send(i, color, None, 0, 0, d2, -1, 5)
        for color in range(2):
            share(i, color, None, 0, 0)

    def second(i, color, b):
        d2 = DIMS[color][1]
        send(i, color, None, OFFS[b], 0, d2, 1, 4 + 4 * b)
        send(i, color, None, OFFS[b], 0, d2, -1, 5 + 4 * b)

    def first_near(i):
        for color, (d1, _) in enumerate(DIMS):
            for side, (off, sign) in enumerate(((-1, 1), (1, -1))):
                take(i, color, None, off, 0, side)
                send(i, color, side, off, 0, d1, sign, 2 + side)
                second(i, color, 1 + side)
                share(i, color, None, off, 0)

    def first_far(i):
        for color in range(2):
            take(i, color, 0, 2, 0, 2)
            take(i, color, 1, 2, 0, 3)
            second(i, color, 3)
            share(i, color, None, 2, 0)

    def second_near(i, blocks):
        for b in blocks:
            for color, (_, d2) in enumerate(DIMS):
                for side, (off, sign) in enumerate(((-1, 1), (1, -1))):
                    take(i, color, None, OFFS[b], off, 4 + 4 * b + side)
                    send(i, color, side, OFFS[b], off, d2, sign, 6 + 4 * b + side)
                    share(i, color, None, OFFS[b], off)

    def second_far(i, blocks):
        for b in blocks:
            for color in range(2):
                take(i, color, 0, OFFS[b], 2, 6 + 4 * b)
                take(i, color, 1, OFFS[b], 2, 7 + 4 * b)
                share(i, color, None, OFFS[b], 2)

    def total(i, blocks):
        n = 8 if i < len(ENV) else CORE[i - len(ENV)][1] // 2
        return core_all.at[pl.ds(0, n), pl.ds(0, 16 * blocks), :]

    def partner_done(i):
        ref = total(i, 16)
        remote(ref, ref, dss.at[i], ds.at[i], partner).wait_recv()

    def sends_done(i):
        ref = total(i, 15)
        remote(ref, ref, ss.at[i], ds.at[i], partner).wait_send()
        ref = total(i, 16)
        remote(ref, ref, dss.at[i], ds.at[i], partner).wait_send()

    n8 = 8 * PAIRS

    def set_weights():
        up = (lax.broadcasted_iota(jnp.int32, (n8, PAIRS), 0) // 8
              == lax.broadcasted_iota(jnp.int32, (n8, PAIRS), 1)).astype(F32).astype(BF16)
        left = jnp.dot(up, wbuf[...], preferred_element_type=F32).astype(BF16)
        full = lax.dot_general(left, up, (((1,), (1,)), ((), ())), preferred_element_type=F32)
        same_row = (lax.rem(lax.broadcasted_iota(jnp.int32, (n8, n8), 0), 8)
                    == lax.rem(lax.broadcasted_iota(jnp.int32, (n8, n8), 1), 8))
        kron[...] = jnp.where(same_row, full, 0.0).astype(BF16)
        run[0] = jnp.zeros((BLK, BLK), F32)

    def mix(lo, count):
        def one(g, carry):
            rows = pl.ds(pl.multiple_of(lo + 16 * g, 16), 16)
            e = env_all[:, :, rows, :]
            parts = [
                jnp.dot(kron[...], e[:, :, 8 * h : 8 * h + 8].reshape(n8, BLK), preferred_element_type=F32)
                for h in range(2)
            ]
            both = jnp.concatenate([m.reshape(PAIRS, 8, BLK) for m in parts], axis=1)
            mixed[:, rows, :] = both.astype(BF16)
            return carry

        lax.fori_loop(0, count // 16, one, 0)

    def pairs(lo, count):
        def four(i, carry):
            for u in range(4):
                k = lo + 4 * i + u
                m = core_all[k]
                h = jnp.dot(mixed[k], m, preferred_element_type=F32).astype(BF16)
                t = lax.dot_general(m, h, (((0,), (0,)), ((), ())), preferred_element_type=F32)
                run[k + 1] = t + run[k] * mscal[0, k].astype(F32)
            return carry

        lax.fori_loop(0, count // 4, four, 0)

    def compute(i, half):
        if i < 0:
            return
        if i < len(ENV):
            mix(ENV[i] + half * (ROWS // 2), ROWS // 2)
        else:
            lo, count = CORE[i - len(ENV)]
            pairs(lo + half * (count // 2), count // 2)

    place_own(range(len(ENV)))

    @pl.when(role == 0)
    def _():
        pltpu.make_async_copy(w_in.at[0], wbuf, meta_r.at[0]).start()
        pltpu.make_async_copy(meta_in, mbuf, meta_r.at[1]).start()
        remote(w_in.at[1], wbuf, meta_s.at[0], meta_r.at[0], partner).start()
        remote(meta_in, mbuf, meta_s.at[1], meta_r.at[1], partner).start()

    start_own(0)
    start_own(1)
    place_own(range(len(ENV), STAGES))
    pltpu.make_async_copy(w_in.at[0], wbuf, meta_r.at[0]).wait()
    pltpu.make_async_copy(meta_in, mbuf, meta_r.at[1]).wait()
    to_scalar = pltpu.make_async_copy(mbuf, mscal, sc_sem)
    to_scalar.start()
    set_weights()
    to_scalar.wait()
    first_near(0)
    for i in range(STAGES + 2):
        if i + 2 < STAGES:
            start_own(i + 2)
        if i + 1 < STAGES:
            first_near(i + 1)
        if i < STAGES:
            second_near(i, (0,))
            first_far(i)
        if 1 <= i <= STAGES:
            second_far(i - 1, (0,))
            second_near(i - 1, (3,))
        compute(i - 3, 0)
        if i < STAGES:
            second_near(i, (1, 2))
        if 1 <= i <= STAGES:
            second_far(i - 1, (1, 2))
        if i >= 2:
            second_far(i - 2, (3,))
        compute(i - 3, 1)
        if i >= 2:
            partner_done(i - 2)
    compute(STAGES - 1, 0)
    compute(STAGES - 1, 1)

    def part(xj, q):
        return run[mscal[0, PAIRS + 4 * xj + q]]

    far, fwd, back = rem(x + 2, 4), rem(x + 1, 4), rem(x - 1, 4)

    def hop(n, q, dst, recv, sign):
        return remote(obuf.at[4 * n + q], dst.at[q], xs.at[4 * n + q], recv.at[q], near["x", sign])

    def to_far(q):
        obuf[q] = part(far, q).astype(BF16)
        hop(0, q, r1, xr1, 1 if q < 2 else -1).start()

    def to_next(q, sign, add):
        value = part(fwd if sign == 1 else back, q)
        n, dst, recv = (1, r2m, xrm) if sign == 1 else (2, r2p, xrp)
        if add:
            hop(0, q, r1, xr1, 1).wait_recv()
            value = value + r1[q].astype(F32)
        obuf[4 * n + q] = value.astype(BF16)
        hop(n, q, dst, recv, sign).start()

    for q in (0, 2, 1, 3):
        to_far(q)
    for b in range(2):
        to_next(2 + b, 1, False)
        to_next(b, -1, False)
        to_next(b, 1, True)
        to_next(2 + b, -1, True)

    def whole(q):
        return part(x, q) + r2m[q].astype(F32) + r2p[q].astype(F32)

    def across_copy(cj, b):
        return remote(zs.at[2 * cj + b], fin_z.at[b], fs.at[cj, b], fr.at[b], across[cj])

    for b in range(2):
        for q in (b, 2 + b):
            hop(1, q, r2m, xrm, 1).wait_recv()
            hop(2, q, r2p, xrp, 1).wait_recv()

        @pl.when(role == 1)
        def _():
            for cj in range(2):
                zs[2 * cj + b] = whole(2 * cj + b).astype(BF16)
                across_copy(cj, b).start()

        @pl.when(role == 0)
        def _():
            fin_s[b] = whole(2 * other + b)
            remote(fin_s.at[b], fin_f.at[b], fs.at[0, b], fd.at[b], partner).start()
            fin_f[b] = whole(2 * c + b)

    for b in range(2):
        across_copy(0, b).wait_recv()

    @pl.when(role == 1)
    def _():
        for b in range(2):
            remote(fin_s.at[b], fin_f.at[b], fs.at[0, b], fd.at[b], partner).wait_recv()

    for i in range(STAGES):
        sends_done(i)
    for n in range(12):
        remote(obuf.at[n], obuf.at[n], xs.at[n], xr1.at[0], partner).wait_send()

    @pl.when(role == 1)
    def _():
        for i in range(STAGES):
            remote(shard(i, None, given), shard(i, t_own, held), own_s.at[i], own.at[i], swap).wait_send()
        for cj in range(2):
            for b in range(2):
                across_copy(cj, b).wait_send()

    @pl.when(role == 0)
    def _():
        remote(w_in.at[1], wbuf, meta_s.at[0], meta_r.at[0], partner).wait_send()
        remote(meta_in, mbuf, meta_s.at[1], meta_r.at[1], partner).wait_send()
        for b in range(2):
            remote(fin_s.at[b], fin_f.at[b], fs.at[0, b], fd.at[b], partner).wait_send()


def per_device(env_blocks, core_blocks, mpo_coeffs, pair_left, pair_right, block_dims):
    term = lax.axis_index("term")
    sec = lax.axis_index("sec")
    ids = jnp.arange(16, dtype=jnp.int32)
    order = jnp.arange(PAIRS, dtype=jnp.int32)
    key = pair_right * PAIRS + order
    rank = jnp.sum((key[None, :] < key[:, None]).astype(jnp.int32), axis=1)
    perm = rank[None, :] == order[:, None]
    left_dim = jnp.sum(jnp.where((sec * 2 + pair_left)[:, None] == ids[None, :], block_dims[None, :], 0), axis=1)
    right_hot = pair_right[:, None] == ids[None, :]
    right_dim = jnp.sum(jnp.where(right_hot, block_dims[None, :], 0), axis=1)
    rows = term * 8 + jnp.arange(8, dtype=jnp.int32)
    cols = jnp.arange(BLK, dtype=jnp.int32)
    keep = (rows[None, :, None] < left_dim[:, None, None]) & (cols[None, None, :] < right_dim[:, None, None])
    masked = jnp.where(keep, core_blocks, jnp.zeros((), BF16))
    hot = perm.astype(BF16)
    core_sorted = jnp.einsum("kp,px->kx", hot, masked.reshape(PAIRS, 8 * BLK), preferred_element_type=F32)
    core_sorted = core_sorted.astype(BF16).reshape(PAIRS, 8, BLK)
    left_hot = (pair_left[:, None] == jnp.arange(2)[None, :]).astype(BF16)

    def weights(v):
        own = lax.dynamic_index_in_dim(mpo_coeffs, v, 1, keepdims=False)
        spread = own.T[:, :, None] * left_hot[:, None, :]
        return jnp.dot(hot, spread.reshape(PAIRS, 64), preferred_element_type=F32).astype(BF16)

    w_both = jnp.stack([weights(term), weights(term + 1 - 2 * lax.rem(term, 2))])
    counts = jnp.sum(right_hot.astype(jnp.int32), axis=0)
    ends = jnp.sum(jnp.where(ids[None, :] <= ids[:, None], counts[None, :], 0), axis=1)
    last = jnp.where(counts > 0, ends, 0)
    firsts = jnp.sum(((ends - counts)[None, :] == order[:, None]) & (counts > 0)[None, :], axis=1)
    same = (1 - firsts).astype(jnp.int32)
    meta = jnp.concatenate([same, last.astype(jnp.int32), jnp.zeros((48,), jnp.int32)]).reshape(1, 128)
    meta = jnp.broadcast_to(meta, (8, 128))
    vmem = pl.BlockSpec(memory_space=pltpu.VMEM)
    dma = pltpu.SemaphoreType.DMA
    block = (BLK, BLK)
    first, second = pl.pallas_call(
        kernel,
        name="sweep_update",
        out_shape=(jax.ShapeDtypeStruct((2, *block), F32), jax.ShapeDtypeStruct((2, *block), BF16)),
        in_specs=[vmem] * 4,
        out_specs=(vmem, vmem),
        scratch_shapes=[
            pltpu.VMEM((32, 2, *block), BF16),
            pltpu.VMEM((PAIRS, *block), BF16),
            pltpu.VMEM((PAIRS, *block), BF16),
            pltpu.VMEM((PAIRS + 1, *block), F32),
            pltpu.VMEM((8 * PAIRS, 8 * PAIRS), BF16),
            pltpu.VMEM((PAIRS, PAIRS), BF16),
            pltpu.VMEM((8, 128), jnp.int32),
            pltpu.SMEM((8, 128), jnp.int32),
            pltpu.VMEM((12, *block), BF16),
            pltpu.VMEM((4, *block), BF16),
            pltpu.VMEM((4, *block), BF16),
            pltpu.VMEM((4, *block), BF16),
            pltpu.VMEM((2, *block), F32),
            pltpu.VMEM((4, *block), BF16),
            dma((STAGES, 2, 20)),
            dma((STAGES,)),
            dma((STAGES,)),
            dma((STAGES,)),
            dma((STAGES,)),
            dma((STAGES,)),
            dma((2,)),
            dma((2,)),
            dma,
            dma((4,)),
            dma((4,)),
            dma((4,)),
            dma((12,)),
            dma((2,)),
            dma((2,)),
            dma((2, 2)),
        ],
        compiler_params=pltpu.CompilerParams(
            collective_id=0, has_side_effects=True, vmem_limit_bytes=64000 * 1024
        ),
    )(env_blocks.reshape(2, *block), core_sorted, w_both, meta)
    return (first + second.astype(F32)).reshape(1, 2, *block)


def solution(mesh):
    return jax.shard_map(
        per_device,
        mesh=mesh,
        in_specs=(
            P("term", "sec", None, None),
            P("sec", "term", None),
            P(None, None, "sec"),
            P("sec"),
            P("sec"),
            P(),
        ),
        out_specs=P("term", "sec", None, None),
        check_vma=False,
    )
```
